32 devices in a mesh: node: 8 (over z, x), rep: 4 (over y, core).
Axes of the slice: x: 2, y: 2, z: 4, core: 2. Of those that a mesh axis runs over, the one named last changes fastest.
Arguments:
- features: bfloat16 [8192, 512], P(('node', 'rep')), may hold values from -6 to 6
- weight: bfloat16 [512, 512], replicated, may hold values from -0.25 to 0.25
- cotangent: bfloat16 [8192, 512], P(('node', 'rep')), may hold values from -6 to 6
- tile_values: bfloat16 [8192, 128, 128], P(('node', 'rep')), may hold values from -0.125 to 0.125
- tile_row: int32 [8192], P(('node', 'rep')), may hold values from 0 to 7
- tile_col: int32 [8192], P(('node', 'rep')), may hold values from 0 to 15
- tile_count: int32 [32], P(('node', 'rep')), may hold values from 64 to 256, as said below
Outputs:
- activation: bfloat16 [8192, 512], P(('node', 'rep'))
- weight_grad: float32 [512, 512], replicated
- feature_grad: bfloat16 [8192, 512], P(('node', 'rep'))
The draws below stay inside these ranges and needn't reach their ends.
Inputs may be any that keep to these rules, and one draw needn't show every extreme that they name: `tile_count`: slots of a device below its count hold tiles, the others are ignored; some device uses all 256 slots.
All inputs are finite; a program needn't handle non-finite values.
Results may differ from the reference program's by a relative error of at most 0.023.
Values may be sent and summed in bfloat16 or wider, within the bound.
A program may use at most 128 MiB of HBM per device.

```python
import math
import jax
import jax.numpy as jnp
from jax import lax

F = 512
TB = 128
ROWS_DEV = 1024
CAP = 256
NODES = 8192
BLOCKS_DEV = 8
SUB_BLOCKS = 2
TILES = 8192
N_NODE = 8
N_REP = 4
DEVICES = 32


def draw_tile_count(key, part):
    counts_drawn = jax.random.randint(key, (DEVICES,), CAP // 4, 3 * CAP // 4 + 1, dtype=jnp.int32)
    busiest = jax.random.randint(jax.random.fold_in(key, 7), (), 0, DEVICES, dtype=jnp.int32)
    return jnp.where(jnp.arange(DEVICES, dtype=jnp.int32) == busiest, CAP, counts_drawn).astype(jnp.int32)


def set_ends(array, key, least, largest):
    extent = array.shape
    spot = [jax.random.randint(jax.random.fold_in(key, axis), (), 0, extent[axis]) for axis in range(len(extent))]
    array = array.at[tuple(spot)].set(least)
    longest = extent.index(max(extent))
    spot[longest] = (spot[longest] + 1) % extent[longest]
    return array.at[tuple(spot)].set(largest)


def level_of(key, extent, pieces, low, high):
    def one(dim, blocks):
        draws = jax.random.uniform(jax.random.fold_in(jax.random.fold_in(key, 6), dim), (blocks,), jnp.float32, low / len(pieces), high / len(pieces))
        return jnp.repeat(jnp.exp(draws), extent[dim] // blocks).reshape((-1,) + (1,) * (len(extent) - dim - 1))

    factor_of = one(*pieces[0])
    for cut in pieces[1:]:
        factor_of = factor_of * one(*cut)
    return factor_of


def bell_draw(key, shape, width, limit, cuts=(), held_as=jnp.bfloat16):
    loudness = level_of(key, shape, cuts, -0.22, 0.18) if cuts else 1.0
    drawn = jax.random.normal(key, shape, jnp.float32) * width * loudness
    return jnp.minimum(jnp.maximum(drawn, -limit), limit).astype(held_as)


def setup_inputs(seed: int = 0) -> dict:
    keys = jax.random.split(jax.random.key(seed), 8)
    return {
        "features": bell_draw(keys[0], (NODES, F), 1.0, 6.0, ((0, 32),)),
        "weight": bell_draw(keys[1], (F, F), F ** -0.5, 0.25),
        "cotangent": bell_draw(keys[2], (NODES, F), 1.0, 6.0, ((0, 32),)),
        "tile_values": bell_draw(keys[3], (TILES, TB, TB), (CAP * TB * TB // (2 * ROWS_DEV)) ** -0.5, 0.125, ((0, 32),)),
        "tile_row": set_ends(jax.random.randint(keys[4], (TILES,), 0, BLOCKS_DEV), jax.random.fold_in(keys[4], 1), 0, BLOCKS_DEV - 1).astype(jnp.int32),
        "tile_col": set_ends(jax.random.randint(keys[5], (TILES,), 0, N_NODE * SUB_BLOCKS), jax.random.fold_in(keys[5], 1), 0, (N_NODE * SUB_BLOCKS) - 1).astype(jnp.int32),
        "tile_count": draw_tile_count(jax.random.fold_in(keys[7], 71), 0),
    }


def smooth_gate(values):
    return jax.nn.gelu(values, approximate=True)

def tile_places(tile_row, tile_col):
    slot_index = jnp.arange(TILES, dtype=jnp.int32)
    device_index = slot_index // CAP
    node_index = device_index // N_REP
    rep_index = device_index % N_REP
    row_blocks = node_index * BLOCKS_DEV + tile_row
    col_blocks = tile_col // SUB_BLOCKS * BLOCKS_DEV + rep_index * SUB_BLOCKS + tile_col % SUB_BLOCKS
    return (row_blocks.astype(jnp.int32), col_blocks.astype(jnp.int32))

def reference(features, weight, cotangent, tile_values, tile_row, tile_col, tile_count):
    row_blocks, col_blocks = tile_places(tile_row, tile_col)
    slot_index = jnp.arange(TILES, dtype=jnp.int32)
    slot_live = (slot_index % CAP < jnp.repeat(tile_count, CAP)).astype(jnp.float32)
    per_device = (tile_values.reshape(DEVICES, CAP, TB, TB), row_blocks.reshape(DEVICES, CAP), col_blocks.reshape(DEVICES, CAP), slot_live.reshape(DEVICES, CAP))
    source_blocks = features.reshape(NODES // TB, TB, F)

    def forward_device(totals, packed):
        values, rows_here, cols_here, slot_mask = packed
        product = jnp.einsum('tij,tjf->tif', values.astype(jnp.float32), source_blocks[cols_here].astype(jnp.float32), precision=lax.Precision.HIGHEST)
        return (totals.at[rows_here].add(product * slot_mask[:, None, None]), None)
    sums = lax.scan(forward_device, jnp.zeros((NODES // TB, TB, F), jnp.float32), per_device)[0]
    aggregate = sums.reshape(NODES, F).astype(jnp.bfloat16)
    pre = jnp.dot(aggregate, weight, preferred_element_type=jnp.float32)
    activated, pullback = jax.vjp(smooth_gate, pre)
    pre_grad = pullback(cotangent.astype(jnp.float32))[0].astype(jnp.bfloat16)
    weight_grad = jnp.dot(aggregate.T, pre_grad, preferred_element_type=jnp.float32) * (1.0 / math.sqrt(NODES))
    row_grad = jnp.dot(pre_grad, weight.T, preferred_element_type=jnp.float32).astype(jnp.bfloat16)
    grad_blocks = row_grad.reshape(NODES // TB, TB, F)

    def backward_device(totals, packed):
        values, rows_here, cols_here, slot_mask = packed
        product = jnp.einsum('tji,tjf->tif', values.astype(jnp.float32), grad_blocks[rows_here].astype(jnp.float32), precision=lax.Precision.HIGHEST)
        return (totals.at[cols_here].add(product * slot_mask[:, None, None]), None)
    back_sums = lax.scan(backward_device, jnp.zeros((NODES // TB, TB, F), jnp.float32), per_device)[0]
    feature_grad = back_sums.reshape(NODES, F).astype(jnp.bfloat16)
    return (activated.astype(jnp.bfloat16), weight_grad, feature_grad)
```

```python
import functools
import math

import jax
import jax.numpy as jnp
from jax import lax
from jax.experimental import pallas as pl
from jax.experimental.pallas import tpu as pltpu
from jax.sharding import PartitionSpec as P

TB = 128


def densify_kernel(blocks, subs, group, rows_ref, cols_ref, count_ref, tiles_ref, out_ref, acc, stage, sems):
    turn = pl.program_id(0)
    places = acc.shape[0] - 1
    nodes = places // (blocks * subs)

    @pl.when(turn == 0)
    def _():
        @pl.loop(0, places)
        def _(p):
            acc[p] = jnp.zeros((TB, TB), jnp.float32)

    count = count_ref[0]

    @pl.when(turn * group < count)
    def _():
        for t in range(group):
            slot = turn * group + t
            col = cols_ref[slot]
            place = (col // subs * blocks + rows_ref[slot]) * subs + col % subs
            place = jnp.where(slot < count, place, places)
            acc[place] += tiles_ref[t].astype(jnp.float32)

    @pl.when(turn == pl.num_programs(0) - 1)
    def _():
        def copy_out(o):
            return pltpu.make_async_copy(stage.at[o % 2], out_ref.at[o], sems.at[o % 2])

        for o in range(nodes):
            if o >= 2:
                copy_out(o - 2).wait()
            for r in range(blocks):
                for s in range(subs):
                    stage[o % 2, r * TB:(r + 1) * TB, s * TB:(s + 1) * TB] = acc[
                        (o * blocks + r) * subs + s
                    ].astype(jnp.bfloat16)
            copy_out(o).start()
        for o in range(max(nodes - 2, 0), nodes):
            copy_out(o).wait()


def densify(tile_values, tile_row, tile_col, tile_count, nodes, blocks, subs):
    slots = tile_values.shape[0]
    group = 16 if slots % 16 == 0 else 1
    places = nodes * blocks * subs

    def tile_block(i, rows, cols, count):
        return (jnp.minimum(i, (count[0] + group - 1) // group - 1), 0, 0)

    return pl.pallas_call(
        functools.partial(densify_kernel, blocks, subs, group),
        out_shape=jax.ShapeDtypeStruct((nodes, blocks * TB, subs * TB), jnp.bfloat16),
        grid_spec=pltpu.PrefetchScalarGridSpec(
            num_scalar_prefetch=3,
            grid=(slots // group,),
            in_specs=[pl.BlockSpec((group, TB, TB), tile_block)],
            out_specs=pl.BlockSpec(memory_space=pl.ANY),
            scratch_shapes=[
                pltpu.VMEM((places + 1, TB, TB), jnp.float32),
                pltpu.VMEM((2, blocks * TB, subs * TB), jnp.bfloat16),
                pltpu.SemaphoreType.DMA((2,)),
            ],
        ),
        compiler_params=pltpu.CompilerParams(vmem_limit_bytes=60 * 1024 * 1024),
        name="densify",
    )(tile_row, tile_col, tile_count, tile_values)


def local(features, weight, cotangent, tile_values, tile_row, tile_col, tile_count):
    rows_quarter, width = features.shape
    rep_count = lax.axis_size("rep")
    node_count = lax.axis_size("node")
    scale = 1.0 / math.sqrt(rows_quarter * rep_count * node_count)
    subs = rows_quarter // TB
    blocks = subs * rep_count
    dense = densify(tile_values, tile_row, tile_col, tile_count, node_count, blocks, subs)
    gathered = lax.all_gather(features, "node", axis=0, tiled=False)
    partial_sum = lax.dot_general(
        dense, gathered, (((0, 2), (0, 1)), ((), ())), preferred_element_type=jnp.float32
    )
    aggregate = lax.psum_scatter(
        partial_sum.astype(jnp.bfloat16), "rep", scatter_dimension=0, tiled=True
    )
    pre = jnp.dot(aggregate, weight, preferred_element_type=jnp.float32)
    activated, pullback = jax.vjp(functools.partial(jax.nn.gelu, approximate=True), pre)
    pre_grad = pullback(cotangent.astype(jnp.float32))[0].astype(jnp.bfloat16)
    row_grad = jnp.dot(pre_grad, weight.T, preferred_element_type=jnp.float32).astype(jnp.bfloat16)
    all_grad = lax.all_gather(row_grad, "rep", axis=0, tiled=True)
    weight_term = jnp.dot(aggregate.T, pre_grad, preferred_element_type=jnp.float32)
    weight_grad = lax.psum(weight_term, ("node", "rep")) * scale
    terms = lax.dot_general(
        dense, all_grad, (((1,), (0,)), ((), ())), preferred_element_type=jnp.float32
    ).astype(jnp.bfloat16)
    feature_grad = lax.psum_scatter(
        terms.reshape(-1, width), "node", scatter_dimension=0, tiled=True
    )
    return (activated.astype(jnp.bfloat16), weight_grad, feature_grad)


def solution(mesh):
    in_specs = (
        P(("node", "rep"), None),
        P(),
        P(("node", "rep"), None),
        P(("node", "rep"), None, None),
        P(("node", "rep")),
        P(("node", "rep")),
        P(("node", "rep")),
    )
    out_specs = (P(("node", "rep"), None), P(), P(("node", "rep"), None))
    return jax.shard_map(local, mesh=mesh, in_specs=in_specs, out_specs=out_specs, check_vma=False)
```

```python
import functools
import math

import jax
import jax.numpy as jnp
from jax import lax
from jax.experimental import pallas as pl
from jax.experimental.pallas import tpu as pltpu
from jax.sharding import PartitionSpec as P

TB = 128


def densify_kernel(blocks, subs, group, rows_ref, cols_ref, count_ref, tiles_ref, out_ref, acc, stage, sems):
    turn = pl.program_id(0)
    places = acc.shape[0] - 1
    nodes = places // (blocks * subs)

    @pl.when(turn == 0)
    def _():
        @pl.loop(0, places)
        def _(p):
            acc[p] = jnp.zeros((TB, TB), jnp.float32)

    count = count_ref[0]

    @pl.when(turn * group < count)
    def _():
        for t in range(group):
            slot = turn * group + t
            col = cols_ref[slot]
            place = (col // subs * blocks + rows_ref[slot]) * subs + col % subs
            place = jnp.where(slot < count, place, places)
            acc[place] += tiles_ref[t].astype(jnp.float32)

    @pl.when(turn == pl.num_programs(0) - 1)
    def _():
        def copy_out(o):
            return pltpu.make_async_copy(stage.at[o % 2], out_ref.at[o], sems.at[o % 2])

        for o in range(nodes):
            if o >= 2:
                copy_out(o - 2).wait()
            for r in range(blocks):
                for s in range(subs):
                    stage[o % 2, r * TB:(r + 1) * TB, s * TB:(s + 1) * TB] = acc[
                        (o * blocks + r) * subs + s
                    ].astype(jnp.bfloat16)
            copy_out(o).start()
        for o in range(max(nodes - 2, 0), nodes):
            copy_out(o).wait()


def densify(tile_values, tile_row, tile_col, tile_count, nodes, blocks, subs):
    slots = tile_values.shape[0]
    group = 16 if slots % 16 == 0 else 1
    places = nodes * blocks * subs

    def tile_block(i, rows, cols, count):
        return (jnp.minimum(i, (count[0] + group - 1) // group - 1), 0, 0)

    return pl.pallas_call(
        functools.partial(densify_kernel, blocks, subs, group),
        out_shape=jax.ShapeDtypeStruct((nodes, blocks * TB, subs * TB), jnp.bfloat16),
        grid_spec=pltpu.PrefetchScalarGridSpec(
            num_scalar_prefetch=3,
            grid=(slots // group,),
            in_specs=[pl.BlockSpec((group, TB, TB), tile_block)],
            out_specs=pl.BlockSpec(memory_space=pl.ANY),
            scratch_shapes=[
                pltpu.VMEM((places + 1, TB, TB), jnp.float32),
                pltpu.VMEM((2, blocks * TB, subs * TB), jnp.bfloat16),
                pltpu.SemaphoreType.DMA((2,)),
            ],
        ),
        compiler_params=pltpu.CompilerParams(vmem_limit_bytes=60 * 1024 * 1024),
        name="densify",
    )(tile_row, tile_col, tile_count, tile_values)


def layer_kernel(
    nodes, inner, scale, feat, cot, weight, dense_hbm, act_out, wg_out, fg_out,
    dense, xbuf, acc, cs, cr, ys, yr, agg, gbuf, wacc, wcs, wcr, wxs, wxr, wys, wyr, wzs, wzr, wfull,
    bown, xs, xr, zs, zr,
    dense_sem, ag_send, ag_recv, c_send, c_recv, y_send, y_recv, g_send, g_recv,
    w_send, w_recv, wz_send, wz_recv, wa_send, wa_recv, x_send, x_recv, z_send, z_recv,
):
    line = nodes // inner
    parts = acc.shape[0]
    rows, width = feat.shape
    cols = width // parts
    node, rep = lax.axis_index("node"), lax.axis_index("rep")
    z, x = node // inner, node % inner
    y, c = rep // 2, rep % 2
    up, down, across = (node + inner, rep), (node - inner, rep), (z * inner + 1 - x, rep)
    mate, over = (node, y * 2 + 1 - c), (node, (1 - y) * 2 + c)
    bf16, f32 = jnp.bfloat16, jnp.float32

    def remote(src, dst, send, recv, device):
        return pltpu.make_async_remote_copy(
            src_ref=src, dst_ref=dst, send_sem=send, recv_sem=recv,
            device_id=device, device_id_type=pl.DeviceIdType.MESH,
        )

    load_dense = pltpu.make_async_copy(dense_hbm, dense, dense_sem)
    load_dense.start()

    barrier = pltpu.get_barrier_semaphore()
    for device in (across, mate, over):
        pl.semaphore_signal(barrier, inc=1, device_id=device, device_id_type=pl.DeviceIdType.MESH)
    for k in range(1, line):
        pl.semaphore_signal(
            barrier, inc=1, device_id=((z + k) % line * inner + x, rep),
            device_id_type=pl.DeviceIdType.MESH,
        )
    pl.semaphore_wait(barrier, 3 + line - 1)

    def ag_copy(way, zz, s, src=None):
        slot = zz * inner + x
        src = xbuf.at[slot, s] if src is None else src
        return remote(
            src, xbuf.at[slot, s], ag_send.at[way, zz, s], ag_recv.at[slot, s], (up, down, across)[way]
        )

    def ag_wait(slot, s):
        remote(xbuf.at[slot, s], xbuf.at[slot, s], ag_send.at[0, 0, s], ag_recv.at[slot, s], across).wait_recv()

    for s in range(parts):
        own = feat.at[:, s * cols:(s + 1) * cols]
        ag_copy(2, z, s, own).start()
        pl.when(z < line - 1)(lambda own=own, s=s: ag_copy(0, z, s, own).start())
        pl.when(z > 0)(lambda own=own, s=s: ag_copy(1, z, s, own).start())

    load_dense.wait()
    chunk = rows

    def multiply(slot, s, block, first=False):
        @pl.loop(0, acc.shape[1] // chunk)
        def _(i):
            here = pl.ds(pl.multiple_of(i * chunk, chunk), chunk)
            term = jnp.dot(dense[slot, here, :], block[...], preferred_element_type=f32)
            if first:
                acc[s, here, :] = term
            else:
                acc[s, here, :] += term

    for s in range(parts):
        multiply(node, s, feat.at[:, s * cols:(s + 1) * cols], True)

    @pl.loop(1, line)
    def _(d):
        low, high = z - d, z + d
        for s in range(parts):
            @pl.when(low >= 0)
            def _():
                ag_wait(low * inner + x, s)
                pl.when(z < line - 1)(lambda: ag_copy(0, low, s).start())
                ag_copy(2, low, s).start()

            @pl.when(high < line)
            def _():
                ag_wait(high * inner + x, s)
                pl.when(z > 0)(lambda: ag_copy(1, high, s).start())
                ag_copy(2, high, s).start()

        for zz, there in ((low, low >= 0), (high, high < line)):
            @pl.when(there)
            def _():
                for s in range(parts):
                    multiply(zz * inner + x, s, xbuf.at[zz * inner + x, s])

    @pl.loop(0, line)
    def _(d):
        low, high = z - d, z + d
        for zz, there in ((low, low >= 0), (high, (high < line) & (d > 0))):
            @pl.when(there)
            def _():
                slot = zz * inner + 1 - x
                for s in range(parts):
                    ag_wait(slot, s)
                    multiply(slot, s, xbuf.at[slot, s])

    def quarter(q):
        return pl.ds(pl.multiple_of(q * rows, rows), rows)

    def c_copy(qy, s):
        return remote(cs.at[qy, s], cr.at[qy, s], c_send.at[qy, s], c_recv.at[qy, s], mate)

    def y_copy(s):
        return remote(ys.at[s], yr.at[s], y_send.at[s], y_recv.at[s], over)

    for qy in (1 - y, y):
        for s in range(parts):
            cs[qy, s] = acc[s, quarter(qy * 2 + 1 - c), :].astype(bf16)
            c_copy(qy, s).start()
    for s in range(parts):
        c_copy(1 - y, s).wait_recv()
        ys[s] = (acc[s, quarter((1 - y) * 2 + c), :] + cr[1 - y, s].astype(f32)).astype(bf16)
        y_copy(s).start()
    for s in range(parts):
        c_copy(y, s).wait_recv()
        y_copy(s).wait_recv()
        total = acc[s, quarter(rep), :] + cr[y, s].astype(f32) + yr[s].astype(f32)
        agg[:, s * cols:(s + 1) * cols] = total.astype(bf16)

    pre = jnp.dot(agg[...], weight[...], preferred_element_type=f32)
    root = math.sqrt(2.0 / math.pi)
    bend = jnp.tanh(root * (pre + 0.044715 * pre * pre * pre))
    act_out[...] = (0.5 * pre * (1.0 + bend)).astype(bf16)
    slope = 0.5 * (1.0 + bend) + 0.5 * pre * (1.0 - bend * bend) * (
        root * (1.0 + 3 * 0.044715 * pre * pre)
    )
    pre_grad = (cot[...].astype(f32) * slope).astype(bf16)
    row_grad = lax.dot_general(
        pre_grad, weight[...], (((1,), (1,)), ((), ())), preferred_element_type=f32
    )
    gbuf[quarter(rep), :] = row_grad.astype(bf16)

    def g_copy(way, q):
        here = gbuf.at[quarter(q), :]
        return remote(here, here, g_send.at[way], g_recv.at[q], (over, mate, mate)[way])

    g_copy(0, rep).start()
    g_copy(1, rep).start()
    wacc[...] = lax.dot_general(
        agg[...], pre_grad, (((0,), (0,)), ((), ())), preferred_element_type=f32
    )
    half = wacc.shape[0] // 2
    fold = half // 2

    def w_copy(step):
        src, dst, device = (
            (wcs, wcr, mate), (wxs, wxr, across), (wys, wyr, over),
            (wfull.at[c, y], wfull.at[c, y], over), (wfull.at[c], wfull.at[c], mate),
        )[step]
        return remote(src, dst, w_send.at[step], w_recv.at[step], device)

    def w_arrival(step):
        dst = (wcr, wxr, wyr, wfull.at[c, 1 - y], wfull.at[1 - c])[step]
        remote(dst, dst, w_send.at[step], w_recv.at[step], mate).wait_recv()

    def part_of(i, size):
        return pl.ds(pl.multiple_of(i * size, size), size)

    wcs[...] = wacc[part_of(1 - c, half), :].astype(bf16)
    w_copy(0).start()
    w_arrival(0)
    wxs[...] = (wacc[part_of(c, half), :] + wcr[...].astype(f32)).astype(bf16)
    w_copy(1).start()
    g_copy(1, y * 2 + 1 - c).wait_recv()
    g_copy(0, (1 - y) * 2 + c).wait_recv()
    g_copy(2, (1 - y) * 2 + c).start()
    w_arrival(1)
    wys[...] = (
        wxs[part_of(1 - y, fold), :].astype(f32) + wxr[part_of(1 - y, fold), :].astype(f32)
    ).astype(bf16)
    w_copy(2).start()
    g_copy(2, (1 - y) * 2 + 1 - c).wait_recv()

    def term_of(slot):
        return lax.dot_general(
            dense[slot], gbuf[...], (((0,), (0,)), ((), ())), preferred_element_type=f32
        )

    def x_copy(zz, s):
        return remote(xs.at[zz, s], xr.at[zz, s], x_send.at[zz, s], x_recv.at[zz, s], across)

    @pl.loop(0, line)
    def _(i):
        d = line - 1 - i
        for zz, there in ((z + d, z + d < line), (z - d, (z - d >= 0) & (d > 0))):
            @pl.when(there)
            def _():
                term = term_of(zz * inner + 1 - x)
                for s in range(parts):
                    xs[zz, s] = term[:, s * cols:(s + 1) * cols].astype(bf16)
                    x_copy(zz, s).start()

    w_arrival(2)
    piece = fold // line
    kept = (
        wxs[part_of(y, fold), :].astype(f32) + wxr[part_of(y, fold), :].astype(f32)
        + wyr[...].astype(f32)
    )
    wzs[...] = kept.reshape(line, piece, width).astype(bf16)

    def wz_copy(k):
        other = (z + k) % line
        return remote(
            wzs.at[other], wzr.at[z], wz_send.at[k], wz_recv.at[z], (other * inner + x, rep)
        )

    def wz_wait(k):
        other = (z + k) % line
        remote(wzr.at[other], wzr.at[other], wz_send.at[k], wz_recv.at[other], across).wait_recv()

    def wa_copy(k):
        other = (z + k) % line
        here = wfull.at[c, y, z]
        return remote(here, here, wa_send.at[k], wa_recv.at[z], (other * inner + x, rep))

    def wa_wait(k):
        other = (z + k) % line
        there = wfull.at[c, y, other]
        remote(there, there, wa_send.at[k], wa_recv.at[other], across).wait_recv()

    for k in range(1, line):
        wz_copy(k).start()

    @pl.loop(0, line)
    def _(zz):
        term = term_of(zz * inner + x)
        for s in range(parts):
            bown[zz, s] = term[:, s * cols:(s + 1) * cols]

    def z_copy(zz, s, slot, device):
        return remote(zs.at[zz, s], zr.at[slot, s], z_send.at[zz, s], z_recv.at[slot, s], device)

    def z_wait(slot, s):
        remote(zr.at[slot, s], zr.at[slot, s], z_send.at[0, s], z_recv.at[slot, s], across).wait_recv()

    def pass_on(i):
        d = line - 1 - i
        for zz, there, inflow, device, slot in (
            (z + d, z + d < line, z > 0, up, z + d),
            (z - d, z - d >= 0, z < line - 1, down, jnp.where(d == 1, line, z - d)),
        ):
            @pl.when(there)
            def _():
                for s in range(parts):
                    x_copy(zz, s).wait_recv()
                    bown[zz, s] += xr[zz, s].astype(f32)

                    @pl.when(inflow)
                    def _():
                        z_wait(zz, s)
                        bown[zz, s] += zr[zz, s].astype(f32)

                    zs[zz, s] = bown[zz, s].astype(bf16)
                    z_copy(zz, s, slot, device).start()

    pass_on(0)
    for k in range(1, line):
        wz_wait(k)
    piece_sum = wzs[z].astype(f32)
    for k in range(1, line):
        piece_sum += wzr[(z + k) % line].astype(f32)
    wfull[c, y, z] = (piece_sum * scale).astype(bf16)
    for k in range(1, line):
        wa_copy(k).start()

    @pl.loop(1, line - 1)
    def _(i):
        pass_on(i)

    for k in range(1, line):
        wa_wait(k)
    w_copy(3).start()
    for s in range(parts):
        x_copy(z, s).wait_recv()
        bown[z, s] += xr[z, s].astype(f32)
    w_arrival(3)
    w_copy(4).start()
    for s in range(parts):
        @pl.when(z > 0)
        def _():
            z_wait(z, s)
            bown[z, s] += zr[z, s].astype(f32)

        @pl.when(z < line - 1)
        def _():
            z_wait(line, s)
            bown[z, s] += zr[line, s].astype(f32)

        fg_out[:, s * cols:(s + 1) * cols] = bown[z, s].astype(bf16)
    w_arrival(4)
    wg_out[...] = wfull[...].astype(f32)

    @pl.loop(0, line)
    def _(zz):
        for s in range(parts):
            pl.when((zz <= z) & (z < line - 1))(lambda: ag_copy(0, zz, s).wait_send())
            pl.when((zz >= z) & (z > 0))(lambda: ag_copy(1, zz, s).wait_send())
            ag_copy(2, zz, s).wait_send()
            x_copy(zz, s).wait_send()
            pl.when(zz != z)(lambda: z_copy(zz, s, zz, across).wait_send())
    for s in range(parts):
        y_copy(s).wait_send()
        for qy in range(2):
            c_copy(qy, s).wait_send()
    for way in range(3):
        g_copy(way, rep).wait_send()
    for step in range(5):
        w_copy(step).wait_send()
    for k in range(1, line):
        wz_copy(k).wait_send()
        wa_copy(k).wait_send()


def layer(features, cotangent, weight, dense, scale, nodes):
    rows, width = features.shape
    inner = 2
    line = nodes // inner
    parts = 2
    cols = width // parts
    all_rows = dense.shape[1]
    half = width // 2
    fold = half // 2
    bf16, f32, dma = jnp.bfloat16, jnp.float32, pltpu.SemaphoreType.DMA
    vmem = pl.BlockSpec(memory_space=pltpu.VMEM)
    shapes = [
        (dense.shape, bf16), ((nodes, parts, rows, cols), bf16), ((parts, all_rows, cols), f32),
        ((2, parts, rows, cols), bf16), ((2, parts, rows, cols), bf16),
        ((parts, rows, cols), bf16), ((parts, rows, cols), bf16),
        ((rows, width), bf16), ((all_rows, width), bf16), ((width, width), f32),
        ((half, width), bf16), ((half, width), bf16), ((half, width), bf16), ((half, width), bf16),
        ((fold, width), bf16), ((fold, width), bf16),
        ((line, fold // line, width), bf16), ((line, fold // line, width), bf16),
        ((2, 2, line, fold // line, width), bf16),
        ((line, parts, rows, cols), f32), ((line, parts, rows, cols), bf16),
        ((line, parts, rows, cols), bf16), ((line, parts, rows, cols), bf16),
        ((line + 1, parts, rows, cols), bf16),
    ]
    sems = [
        dma, dma((3, line, parts)), dma((nodes, parts)), dma((2, parts)), dma((2, parts)),
        dma((parts,)), dma((parts,)), dma((3,)), dma((4,)), dma((5,)), dma((5,)),
        dma((line,)), dma((line,)), dma((line,)), dma((line,)),
        dma((line, parts)), dma((line, parts)), dma((line, parts)), dma((line + 1, parts)),
    ]
    activation, weight_grad, feature_grad = pl.pallas_call(
        functools.partial(layer_kernel, nodes, inner, scale),
        out_shape=(
            jax.ShapeDtypeStruct((rows, width), bf16),
            jax.ShapeDtypeStruct((2, 2, line, fold // line, width), f32),
            jax.ShapeDtypeStruct((rows, width), bf16),
        ),
        in_specs=[vmem, vmem, vmem, pl.BlockSpec(memory_space=pl.ANY)],
        out_specs=(vmem, vmem, vmem),
        scratch_shapes=[pltpu.VMEM(*shape) for shape in shapes] + sems,
        compiler_params=pltpu.CompilerParams(
            collective_id=0, has_side_effects=True, vmem_limit_bytes=63 * 1024 * 1024
        ),
        name="layer",
    )(features, cotangent, weight, dense)
    return activation, weight_grad.reshape(width, width), feature_grad


def local(features, weight, cotangent, tile_values, tile_row, tile_col, tile_count):
    rows_quarter = features.shape[0]
    rep_count = lax.axis_size("rep")
    node_count = lax.axis_size("node")
    scale = 1.0 / math.sqrt(rows_quarter * rep_count * node_count)
    subs = rows_quarter // TB
    blocks = subs * rep_count
    dense = densify(tile_values, tile_row, tile_col, tile_count, node_count, blocks, subs)
    return layer(features, cotangent, weight, dense, scale, node_count)


def solution(mesh):
    in_specs = (
        P(("node", "rep"), None),
        P(),
        P(("node", "rep"), None),
        P(("node", "rep"), None, None),
        P(("node", "rep")),
        P(("node", "rep")),
        P(("node", "rep")),
    )
    out_specs = (P(("node", "rep"), None), P(), P(("node", "rep"), None))
    return jax.shard_map(local, mesh=mesh, in_specs=in_specs, out_specs=out_specs, check_vma=False)
```

```python
import functools
import math

import jax
import jax.numpy as jnp
from jax import lax
from jax.experimental import pallas as pl
from jax.experimental.pallas import tpu as pltpu
from jax.sharding import PartitionSpec as P

TB = 128


def densify_kernel(blocks, subs, group, rows_ref, cols_ref, count_ref, tiles_ref, out_ref, acc, stage, sems):
    turn = pl.program_id(0)
    places = acc.shape[0] - 1
    nodes = places // (blocks * subs)

    @pl.when(turn == 0)
    def _():
        @pl.loop(0, places)
        def _(p):
            acc[p] = jnp.zeros((TB, TB), jnp.float32)

    count = count_ref[0]

    @pl.when(turn * group < count)
    def _():
        @pl.loop(0, group, unroll=True)
        def _(t):
            slot = turn * group + t
            col = cols_ref[slot]
            place = (col // subs * blocks + rows_ref[slot]) * subs + col % subs
            place = jnp.where(slot < count, place, places)
            acc[place] += tiles_ref[t].astype(jnp.float32)

    @pl.when(turn == pl.num_programs(0) - 1)
    def _():
        def copy_out(o):
            return pltpu.make_async_copy(stage.at[o % 2], out_ref.at[o], sems.at[o % 2])

        for o in range(nodes):
            if o >= 2:
                copy_out(o - 2).wait()
            for r in range(blocks):
                for s in range(subs):
                    stage[o % 2, r * TB:(r + 1) * TB, s * TB:(s + 1) * TB] = acc[
                        (o * blocks + r) * subs + s
                    ].astype(jnp.bfloat16)
            copy_out(o).start()
        for o in range(max(nodes - 2, 0), nodes):
            copy_out(o).wait()


def densify(tile_values, tile_row, tile_col, tile_count, nodes, blocks, subs):
    slots = tile_values.shape[0]
    group = math.gcd(slots, 32)
    places = nodes * blocks * subs

    def tile_block(i, rows, cols, count):
        return (jnp.minimum(i, (count[0] + group - 1) // group - 1), 0, 0)

    return pl.pallas_call(
        functools.partial(densify_kernel, blocks, subs, group),
        out_shape=jax.ShapeDtypeStruct((nodes, blocks * TB, subs * TB), jnp.bfloat16),
        grid_spec=pltpu.PrefetchScalarGridSpec(
            num_scalar_prefetch=3,
            grid=(slots // group,),
            in_specs=[pl.BlockSpec((group, TB, TB), tile_block)],
            out_specs=pl.BlockSpec(memory_space=pl.ANY),
            scratch_shapes=[
                pltpu.VMEM((places + 1, TB, TB), jnp.float32),
                pltpu.VMEM((2, blocks * TB, subs * TB), jnp.bfloat16),
                pltpu.SemaphoreType.DMA((2,)),
            ],
        ),
        compiler_params=pltpu.CompilerParams(vmem_limit_bytes=60 * 1024 * 1024),
        cost_estimate=pl.CostEstimate(
            flops=slots * TB * TB, bytes_accessed=4 * slots * TB * TB, transcendentals=0
        ),
        name="densify",
    )(tile_row, tile_col, tile_count, tile_values)


def layer_kernel(
    nodes, inner, scale, feat, feat_x, feat_low, feat_high, cot, weight, dense_hbm, act_out, wg_out, fg_out,
    dense, xbuf, acc, cs, cr, ys, yr, agg, gbuf, wacc, wcs, wcr, wxs, wxr, wys, wyr, wzs, wzr, wfull,
    bown, xs, xr, zs, zr,
    dense_sem, ag_send, ag_recv, c_send, c_recv, y_send, y_recv, g_send, g_recv,
    w_send, w_recv, wz_send, wz_recv, wa_send, wa_recv, x_send, x_recv, z_send, z_recv,
):
    line = nodes // inner
    parts = acc.shape[0]
    rows, width = feat.shape
    cols = width // parts
    node, rep = lax.axis_index("node"), lax.axis_index("rep")
    z, x = node // inner, node % inner
    y, c = rep // 2, rep % 2
    up, down, across = (node + inner, rep), (node - inner, rep), (z * inner + 1 - x, rep)
    mate, over = (node, y * 2 + 1 - c), (node, (1 - y) * 2 + c)
    bf16, f32 = jnp.bfloat16, jnp.float32

    def remote(src, dst, send, recv, device):
        return pltpu.make_async_remote_copy(
            src_ref=src, dst_ref=dst, send_sem=send, recv_sem=recv,
            device_id=device, device_id_type=pl.DeviceIdType.MESH,
        )

    load_dense = pltpu.make_async_copy(dense_hbm, dense, dense_sem)
    load_dense.start()

    barrier = pltpu.get_barrier_semaphore()
    for device in (across, mate, over):
        pl.semaphore_signal(barrier, inc=1, device_id=device, device_id_type=pl.DeviceIdType.MESH)
    for k in range(1, line):
        pl.semaphore_signal(
            barrier, inc=1, device_id=((z + k) % line * inner + x, rep),
            device_id_type=pl.DeviceIdType.MESH,
        )
    pl.semaphore_wait(barrier, 3 + line - 1)

    def ag_copy(way, zz, s, src=None):
        slot = zz * inner + x
        src = xbuf.at[slot, s] if src is None else src
        return remote(
            src, xbuf.at[slot, s], ag_send.at[way, zz, s], ag_recv.at[slot, s], (up, down, across)[way]
        )

    def ag_wait(slot, s):
        remote(xbuf.at[slot, s], xbuf.at[slot, s], ag_send.at[0, 0, s], ag_recv.at[slot, s], across).wait_recv()

    def columns(ref, s):
        return ref.at[:, s * cols:(s + 1) * cols]

    for s in range(parts):
        low_part, high_part = columns(feat_low, s), columns(feat_high, s)

        @pl.when(z > 0)
        def _():
            pl.when(z < line - 1)(lambda: ag_copy(0, z - 1, s, low_part).start())
            ag_copy(2, z - 1, s, low_part).start()

        @pl.when(z < line - 1)
        def _():
            pl.when(z > 0)(lambda: ag_copy(1, z + 1, s, high_part).start())
            ag_copy(2, z + 1, s, high_part).start()

    load_dense.wait()
    chunk = rows

    def multiply(slot, s, block, first=False):
        @pl.loop(0, acc.shape[1] // chunk)
        def _(i):
            here = pl.ds(pl.multiple_of(i * chunk, chunk), chunk)
            term = jnp.dot(dense[slot, here, :], block[...], preferred_element_type=f32)
            if first:
                acc[s, here, :] = term
            else:
                acc[s, here, :] += term

    for s in range(parts):
        multiply(node, s, columns(feat, s), True)
        multiply(z * inner + 1 - x, s, columns(feat_x, s))
        pl.when(z > 0)(lambda s=s: multiply(node - inner, s, columns(feat_low, s)))
        pl.when(z < line - 1)(lambda s=s: multiply(node + inner, s, columns(feat_high, s)))

    @pl.loop(2, line)
    def _(d):
        low, high = z - d, z + d
        for s in range(parts):
            @pl.when(low >= 0)
            def _():
                ag_wait(low * inner + x, s)
                pl.when(z < line - 1)(lambda: ag_copy(0, low, s).start())
                ag_copy(2, low, s).start()

            @pl.when(high < line)
            def _():
                ag_wait(high * inner + x, s)
                pl.when(z > 0)(lambda: ag_copy(1, high, s).start())
                ag_copy(2, high, s).start()

        for zz, there in ((low, low >= 0), (high, high < line)):
            @pl.when(there)
            def _():
                for s in range(parts):
                    multiply(zz * inner + x, s, xbuf.at[zz * inner + x, s])

    def multiply_across(d, s):
        for zz, there in ((z - d, z - d >= 0), (z + d, z + d < line)):
            @pl.when(there)
            def _():
                slot = zz * inner + 1 - x
                ag_wait(slot, s)
                multiply(slot, s, xbuf.at[slot, s])

    @pl.loop(1, line - 1)
    def _(d):
        for s in range(parts):
            multiply_across(d, s)

    def quarter(q):
        return pl.ds(pl.multiple_of(q * rows, rows), rows)

    def c_copy(qy, s):
        return remote(cs.at[qy, s], cr.at[qy, s], c_send.at[qy, s], c_recv.at[qy, s], mate)

    def y_copy(s):
        return remote(ys.at[s], yr.at[s], y_send.at[s], y_recv.at[s], over)

    for s in range(parts):
        multiply_across(line - 1, s)
        for qy in (1 - y, y):
            cs[qy, s] = acc[s, quarter(qy * 2 + 1 - c), :].astype(bf16)
            c_copy(qy, s).start()
        c_copy(1 - y, s).wait_recv()
        ys[s] = (acc[s, quarter((1 - y) * 2 + c), :] + cr[1 - y, s].astype(f32)).astype(bf16)
        y_copy(s).start()
    for s in range(parts):
        c_copy(y, s).wait_recv()
        y_copy(s).wait_recv()
        total = acc[s, quarter(rep), :] + cr[y, s].astype(f32) + yr[s].astype(f32)
        agg[:, s * cols:(s + 1) * cols] = total.astype(bf16)

    pre = jnp.dot(agg[...], weight[...], preferred_element_type=f32)
    root = math.sqrt(2.0 / math.pi)
    bend = jnp.tanh(root * (pre + 0.044715 * pre * pre * pre))
    act_out[...] = (0.5 * pre * (1.0 + bend)).astype(bf16)
    slope = 0.5 * (1.0 + bend) + 0.5 * pre * (1.0 - bend * bend) * (
        root * (1.0 + 3 * 0.044715 * pre * pre)
    )
    pre_grad = (cot[...].astype(f32) * slope).astype(bf16)
    row_grad = lax.dot_general(
        pre_grad, weight[...], (((1,), (1,)), ((), ())), preferred_element_type=f32
    )
    for s in range(parts):
        gbuf[s, quarter(rep), :] = row_grad[:, s * cols:(s + 1) * cols].astype(bf16)

    def g_copy(way, q, s):
        here = gbuf.at[s, quarter(q), :]
        return remote(here, here, g_send.at[way, s], g_recv.at[q, s], (over, mate, mate)[way])

    for s in range(parts):
        g_copy(0, rep, s).start()
    for s in range(parts):
        g_copy(1, rep, s).start()
    wacc[...] = lax.dot_general(
        agg[...], pre_grad, (((0,), (0,)), ((), ())), preferred_element_type=f32
    )
    half = wacc.shape[0] // 2
    strip = half // line

    def w_copy(step):
        src, dst, device = (
            (wcs, wcr, mate), (wys.at[1 - y], wyr, over), (wxs, wxr, across),
            (wfull.at[c, z, y], wfull.at[c, z, y], over), (wfull.at[c], wfull.at[c], mate),
        )[step]
        return remote(src, dst, w_send.at[step], w_recv.at[step], device)

    def w_arrival(step):
        dst = (wcr, wyr, wxr, wfull.at[c, z, 1 - y], wfull.at[1 - c])[step]
        remote(dst, dst, w_send.at[step], w_recv.at[step], mate).wait_recv()

    def wz_copy(k):
        other = (z + k) % line
        return remote(
            wzs.at[other], wzr.at[z], wz_send.at[k], wz_recv.at[z], (other * inner + x, rep)
        )

    def wz_wait(k):
        other = (z + k) % line
        remote(wzr.at[other], wzr.at[other], wz_send.at[k], wz_recv.at[other], across).wait_recv()

    def wa_copy(k):
        other = (z + k) % line
        here = wfull.at[c, z]
        return remote(here, here, wa_send.at[k], wa_recv.at[z], (other * inner + x, rep))

    def wa_wait(k):
        other = (z + k) % line
        there = wfull.at[c, other]
        remote(there, there, wa_send.at[k], wa_recv.at[other], across).wait_recv()

    def half_of(i):
        return pl.ds(pl.multiple_of(i * half, half), half)

    wcs[...] = wacc[half_of(1 - c), :].astype(bf16)
    w_copy(0).start()
    w_arrival(0)
    wzs[...] = (wacc[half_of(c), :] + wcr[...].astype(f32)).reshape(line, strip, width).astype(bf16)
    for k in range(1, line):
        wz_copy(k).start()

    def term_of(slot, s):
        return lax.dot_general(
            dense[slot], gbuf[s], (((0,), (0,)), ((), ())), preferred_element_type=f32
        )

    def x_copy(zz, s):
        return remote(xs.at[zz, s], xr.at[zz, s], x_send.at[zz, s], x_recv.at[zz, s], across)

    def send_across(s):
        @pl.loop(0, line)
        def _(i):
            d = line - 1 - i
            for zz, there in ((z + d, z + d < line), (z - d, (z - d >= 0) & (d > 0))):
                @pl.when(there)
                def _():
                    xs[zz, s] = term_of(zz * inner + 1 - x, s).astype(bf16)
                    x_copy(zz, s).start()

    def own_terms(s):
        @pl.loop(0, line)
        def _(zz):
            bown[zz, s] = term_of(zz * inner + x, s)

    def z_copy(zz, s, slot, device):
        return remote(zs.at[zz, s], zr.at[slot, s], z_send.at[zz, s], z_recv.at[slot, s], device)

    def z_wait(slot, s):
        remote(zr.at[slot, s], zr.at[slot, s], z_send.at[0, s], z_recv.at[slot, s], across).wait_recv()

    def pass_on(d, s):
        for zz, there, inflow, device, slot in (
            (z + d, z + d < line, z > 0, up, z + d),
            (z - d, z - d >= 0, z < line - 1, down, jnp.where(d == 1, line, z - d)),
        ):
            @pl.when(there)
            def _():
                x_copy(zz, s).wait_recv()
                bown[zz, s] += xr[zz, s].astype(f32)

                @pl.when(inflow)
                def _():
                    z_wait(zz, s)
                    bown[zz, s] += zr[zz, s].astype(f32)

                zs[zz, s] = bown[zz, s].astype(bf16)
                z_copy(zz, s, slot, device).start()

    def pass_rest(s):
        @pl.loop(1, line - 1)
        def _(i):
            pass_on(line - 1 - i, s)

    def finish(s):
        x_copy(z, s).wait_recv()
        bown[z, s] += xr[z, s].astype(f32)

        @pl.when(z > 0)
        def _():
            z_wait(z, s)
            bown[z, s] += zr[z, s].astype(f32)

        @pl.when(z < line - 1)
        def _():
            z_wait(line, s)
            bown[z, s] += zr[line, s].astype(f32)

        fg_out[:, s * cols:(s + 1) * cols] = bown[z, s].astype(bf16)

    def gather_grad(s):
        g_copy(1, y * 2 + 1 - c, s).wait_recv()
        g_copy(0, (1 - y) * 2 + c, s).wait_recv()
        g_copy(2, (1 - y) * 2 + c, s).start()

    def rest_of_grad(s):
        g_copy(2, (1 - y) * 2 + 1 - c, s).wait_recv()

    last = parts - 1
    for s in range(last):
        gather_grad(s)
        rest_of_grad(s)
        send_across(s)
        if s == 0:
            gather_grad(last)
        own_terms(s)
        pass_on(line - 1, s)
    for k in range(1, line):
        wz_wait(k)
    total = wzs[z].astype(f32)
    for k in range(1, line):
        total += wzr[(z + k) % line].astype(f32)
    wys[...] = total.reshape(2, strip // 2, width).astype(bf16)
    w_copy(1).start()
    rest_of_grad(last)
    w_arrival(1)
    wxs[...] = (wys[y].astype(f32) + wyr[...].astype(f32)).astype(bf16)
    w_copy(2).start()
    send_across(last)
    own_terms(last)
    for s in range(last):
        pass_rest(s)
    w_arrival(2)
    wfull[c, z, y] = ((wxs[...].astype(f32) + wxr[...].astype(f32)) * scale).astype(bf16)
    w_copy(3).start()
    for s in range(last):
        finish(s)
    pass_on(line - 1, last)
    w_arrival(3)
    for k in range(1, line):
        wa_copy(k).start()
    pass_rest(last)
    for k in range(1, line):
        wa_wait(k)
    w_copy(4).start()
    finish(last)
    w_arrival(4)
    wg_out[...] = wfull[...]

    @pl.loop(0, line)
    def _(zz):
        for s in range(parts):
            pl.when((zz < z) & (z < line - 1))(lambda: ag_copy(0, zz, s).wait_send())
            pl.when((zz > z) & (z > 0))(lambda: ag_copy(1, zz, s).wait_send())
            pl.when(zz != z)(lambda: ag_copy(2, zz, s).wait_send())
            x_copy(zz, s).wait_send()
            pl.when(zz != z)(lambda: z_copy(zz, s, zz, across).wait_send())
    for s in range(parts):
        y_copy(s).wait_send()
        for qy in range(2):
            c_copy(qy, s).wait_send()
        for way in range(3):
            g_copy(way, rep, s).wait_send()
    for step in range(5):
        w_copy(step).wait_send()
    for k in range(1, line):
        wz_copy(k).wait_send()
        wa_copy(k).wait_send()


def finish_kernel(a_ref, w_ref, f_ref, a_out, w_out, f_out):
    a_out[...] = a_ref[...]
    w_out[...] = w_ref[...].astype(jnp.float32)
    f_out[...] = f_ref[...]


def layer(features, hops, cotangent, weight, dense, scale, nodes):
    rows, width = features.shape
    inner = 2
    line = nodes // inner
    parts = 2
    cols = width // parts
    all_rows = dense.shape[1]
    half = width // 2
    strip = half // line
    bf16, f32, dma = jnp.bfloat16, jnp.float32, pltpu.SemaphoreType.DMA
    vmem = pl.BlockSpec(memory_space=pltpu.VMEM)
    shapes = [
        (dense.shape, bf16), ((nodes, parts, rows, cols), bf16), ((parts, all_rows, cols), f32),
        ((2, parts, rows, cols), bf16), ((2, parts, rows, cols), bf16),
        ((parts, rows, cols), bf16), ((parts, rows, cols), bf16),
        ((rows, width), bf16), ((parts, all_rows, cols), bf16), ((width, width), f32),
        ((half, width), bf16), ((half, width), bf16),
        ((strip // 2, width), bf16), ((strip // 2, width), bf16),
        ((2, strip // 2, width), bf16), ((strip // 2, width), bf16),
        ((line, strip, width), bf16), ((line, strip, width), bf16),
        ((2, line, 2, strip // 2, width), bf16),
        ((line, parts, rows, cols), f32), ((line, parts, rows, cols), bf16),
        ((line, parts, rows, cols), bf16), ((line, parts, rows, cols), bf16),
        ((line + 1, parts, rows, cols), bf16),
    ]
    sems = [
        dma, dma((3, line, parts)), dma((nodes, parts)), dma((2, parts)), dma((2, parts)),
        dma((parts,)), dma((parts,)), dma((3, parts)), dma((4, parts)), dma((5,)), dma((5,)),
        dma((line,)), dma((line,)), dma((line,)), dma((line,)),
        dma((line, parts)), dma((line, parts)), dma((line, parts)), dma((line + 1, parts)),
    ]
    held = sum(math.prod(shape) * jnp.dtype(kind).itemsize for shape, kind in shapes)
    activation, weight_grad, feature_grad = pl.pallas_call(
        functools.partial(layer_kernel, nodes, inner, scale),
        out_shape=(
            jax.ShapeDtypeStruct((rows, width), bf16),
            jax.ShapeDtypeStruct((2, line, 2, strip // 2, width), bf16),
            jax.ShapeDtypeStruct((rows, width), bf16),
        ),
        in_specs=[vmem] * 6 + [pl.BlockSpec(memory_space=pl.ANY)],
        out_specs=(vmem, vmem, vmem),
        scratch_shapes=[pltpu.VMEM(*shape) for shape in shapes] + sems,
        compiler_params=pltpu.CompilerParams(
            collective_id=0, has_side_effects=True, vmem_limit_bytes=min(held + (10 << 20), 63 << 20)
        ),
        name="layer",
    )(features, *hops, cotangent, weight, dense)
    return pl.pallas_call(
        finish_kernel,
        out_shape=(
            jax.ShapeDtypeStruct((rows, width), bf16),
            jax.ShapeDtypeStruct((width, width), f32),
            jax.ShapeDtypeStruct((rows, width), bf16),
        ),
        in_specs=[vmem] * 3,
        out_specs=(vmem, vmem, vmem),
        name="finish",
    )(activation, weight_grad.reshape(width, width), feature_grad)


def local(features, weight, cotangent, tile_values, tile_row, tile_col, tile_count):
    rows_quarter = features.shape[0]
    rep_count = lax.axis_size("rep")
    node_count = lax.axis_size("node")
    scale = 1.0 / math.sqrt(rows_quarter * rep_count * node_count)
    subs = rows_quarter // TB
    blocks = subs * rep_count
    inner = 2
    steps = (
        [(n, n ^ 1) for n in range(node_count)],
        [(n, n + inner) for n in range(node_count - inner)],
        [(n, n - inner) for n in range(inner, node_count)],
    )
    hops = [lax.ppermute(features, "node", step) for step in steps]
    dense = densify(tile_values, tile_row, tile_col, tile_count, node_count, blocks, subs)
    return layer(features, hops, cotangent, weight, dense, scale, node_count)


def solution(mesh):
    in_specs = (
        P(("node", "rep"), None),
        P(),
        P(("node", "rep"), None),
        P(("node", "rep"), None, None),
        P(("node", "rep")),
        P(("node", "rep")),
        P(("node", "rep")),
    )
    out_specs = (P(("node", "rep"), None), P(), P(("node", "rep"), None))
    return jax.shard_map(local, mesh=mesh, in_specs=in_specs, out_specs=out_specs, check_vma=False)
```

```python
import functools
import math

import jax
import jax.numpy as jnp
from jax import lax
from jax.experimental import pallas as pl
from jax.experimental.pallas import tpu as pltpu
from jax.sharding import PartitionSpec as P

TB = 128


def densify_kernel(blocks, subs, group, rows_ref, cols_ref, count_ref, tiles_ref, out_ref, acc, stage, sems):
    turn = pl.program_id(0)
    places = acc.shape[0] - 1
    nodes = places // (blocks * subs)

    @pl.when(turn == 0)
    def _():
        @pl.loop(0, places)
        def _(p):
            acc[p] = jnp.zeros((TB, TB), jnp.float32)

    count = count_ref[0]

    @pl.when(turn * group < count)
    def _():
        @pl.loop(0, group, unroll=True)
        def _(t):
            slot = turn * group + t
            col = cols_ref[slot]
            place = (col // subs * blocks + rows_ref[slot]) * subs + col % subs
            place = jnp.where(slot < count, place, places)
            acc[place] += tiles_ref[t].astype(jnp.float32)

    @pl.when(turn == pl.num_programs(0) - 1)
    def _():
        def copy_out(o):
            return pltpu.make_async_copy(stage.at[o % 2], out_ref.at[o], sems.at[o % 2])

        for o in range(nodes):
            if o >= 2:
                copy_out(o - 2).wait()
            for r in range(blocks):
                for s in range(subs):
                    stage[o % 2, r * TB:(r + 1) * TB, s * TB:(s + 1) * TB] = acc[
                        (o * blocks + r) * subs + s
                    ].astype(jnp.bfloat16)
            copy_out(o).start()
        for o in range(max(nodes - 2, 0), nodes):
            copy_out(o).wait()


def densify(tile_values, tile_row, tile_col, tile_count, nodes, blocks, subs):
    slots = tile_values.shape[0]
    group = math.gcd(slots, 32)
    places = nodes * blocks * subs

    def tile_block(i, rows, cols, count):
        return (jnp.minimum(i, (count[0] + group - 1) // group - 1), 0, 0)

    return pl.pallas_call(
        functools.partial(densify_kernel, blocks, subs, group),
        out_shape=jax.ShapeDtypeStruct((nodes, blocks * TB, subs * TB), jnp.bfloat16),
        grid_spec=pltpu.PrefetchScalarGridSpec(
            num_scalar_prefetch=3,
            grid=(slots // group,),
            in_specs=[pl.BlockSpec((group, TB, TB), tile_block)],
            out_specs=pl.BlockSpec(memory_space=pl.ANY),
            scratch_shapes=[
                pltpu.VMEM((places + 1, TB, TB), jnp.float32),
                pltpu.VMEM((2, blocks * TB, subs * TB), jnp.bfloat16),
                pltpu.SemaphoreType.DMA((2,)),
            ],
        ),
        compiler_params=pltpu.CompilerParams(vmem_limit_bytes=60 * 1024 * 1024),
        cost_estimate=pl.CostEstimate(
            flops=slots * TB * TB, bytes_accessed=4 * slots * TB * TB, transcendentals=0
        ),
        name="densify",
    )(tile_row, tile_col, tile_count, tile_values)


def layer_kernel(
    nodes, inner, scale, feat, cot, weight, dense_hbm, act_out, wg_out, fg_out,
    dense, xbuf, acc, cs, cr, ys, yr, agg, gbuf, wacc, wcs, wcr, wxs, wxr, wys, wyr, wzs, wzr, wfull,
    bown, xs, xr, zs, zr,
    dense_sem, ag_send, ag_recv, c_send, c_recv, y_send, y_recv, g_send, g_recv,
    w_send, w_recv, wz_send, wz_recv, wa_send, wa_recv, x_send, x_recv, z_send, z_recv,
):
    line = nodes // inner
    parts = acc.shape[0]
    rows, width = feat.shape
    cols = width // parts
    node, rep = lax.axis_index("node"), lax.axis_index("rep")
    z, x = node // inner, node % inner
    y, c = rep // 2, rep % 2
    up, down, across = (node + inner, rep), (node - inner, rep), (z * inner + 1 - x, rep)
    mate, over = (node, y * 2 + 1 - c), (node, (1 - y) * 2 + c)
    bf16, f32 = jnp.bfloat16, jnp.float32

    def remote(src, dst, send, recv, device):
        return pltpu.make_async_remote_copy(
            src_ref=src, dst_ref=dst, send_sem=send, recv_sem=recv,
            device_id=device, device_id_type=pl.DeviceIdType.MESH,
        )

    load_dense = pltpu.make_async_copy(dense_hbm, dense, dense_sem)
    load_dense.start()

    barrier = pltpu.get_barrier_semaphore()
    for device in (across, mate, over):
        pl.semaphore_signal(barrier, inc=1, device_id=device, device_id_type=pl.DeviceIdType.MESH)
    for k in range(1, line):
        pl.semaphore_signal(
            barrier, inc=1, device_id=((z + k) % line * inner + x, rep),
            device_id_type=pl.DeviceIdType.MESH,
        )
    pl.semaphore_wait(barrier, 3 + line - 1)

    def ag_copy(way, zz, s, src=None):
        slot = zz * inner + x
        src = xbuf.at[slot, s] if src is None else src
        return remote(
            src, xbuf.at[slot, s], ag_send.at[way, zz, s], ag_recv.at[slot, s], (up, down, across)[way]
        )

    def ag_wait(slot, s):
        remote(xbuf.at[slot, s], xbuf.at[slot, s], ag_send.at[0, 0, s], ag_recv.at[slot, s], across).wait_recv()

    def columns(ref, s):
        return ref.at[:, s * cols:(s + 1) * cols]

    for s in range(parts):
        own = columns(feat, s)
        ag_copy(2, z, s, own).start()
        pl.when(z < line - 1)(lambda own=own, s=s: ag_copy(0, z, s, own).start())
        pl.when(z > 0)(lambda own=own, s=s: ag_copy(1, z, s, own).start())

    load_dense.wait()
    chunk = rows

    def multiply(slot, s, block, first=False):
        @pl.loop(0, acc.shape[1] // chunk)
        def _(i):
            here = pl.ds(pl.multiple_of(i * chunk, chunk), chunk)
            term = jnp.dot(dense[slot, here, :], block[...], preferred_element_type=f32)
            if first:
                acc[s, here, :] = term
            else:
                acc[s, here, :] += term

    for s in range(parts):
        multiply(node, s, columns(feat, s), True)

    @pl.loop(1, line)
    def _(d):
        low, high = z - d, z + d
        for s in range(parts):
            @pl.when(low >= 0)
            def _():
                ag_wait(low * inner + x, s)
                pl.when(z < line - 1)(lambda: ag_copy(0, low, s).start())
                ag_copy(2, low, s).start()

            @pl.when(high < line)
            def _():
                ag_wait(high * inner + x, s)
                pl.when(z > 0)(lambda: ag_copy(1, high, s).start())
                ag_copy(2, high, s).start()

        for zz, there in ((low, low >= 0), (high, high < line)):
            @pl.when(there)
            def _():
                for s in range(parts):
                    multiply(zz * inner + x, s, xbuf.at[zz * inner + x, s])

    def multiply_across(d, s):
        for zz, there in ((z - d, z - d >= 0), (z + d, (z + d < line) & (d > 0))):
            @pl.when(there)
            def _():
                slot = zz * inner + 1 - x
                ag_wait(slot, s)
                multiply(slot, s, xbuf.at[slot, s])

    @pl.loop(0, line - 1)
    def _(d):
        for s in range(parts):
            multiply_across(d, s)

    def quarter(q):
        return pl.ds(pl.multiple_of(q * rows, rows), rows)

    def c_copy(qy, s):
        return remote(cs.at[qy, s], cr.at[qy, s], c_send.at[qy, s], c_recv.at[qy, s], mate)

    def y_copy(s):
        return remote(ys.at[s], yr.at[s], y_send.at[s], y_recv.at[s], over)

    for s in range(parts):
        multiply_across(line - 1, s)
        for qy in (1 - y, y):
            cs[qy, s] = acc[s, quarter(qy * 2 + 1 - c), :].astype(bf16)
            c_copy(qy, s).start()
        c_copy(1 - y, s).wait_recv()
        ys[s] = (acc[s, quarter((1 - y) * 2 + c), :] + cr[1 - y, s].astype(f32)).astype(bf16)
        y_copy(s).start()
    for s in range(parts):
        c_copy(y, s).wait_recv()
        y_copy(s).wait_recv()
        total = acc[s, quarter(rep), :] + cr[y, s].astype(f32) + yr[s].astype(f32)
        agg[:, s * cols:(s + 1) * cols] = total.astype(bf16)

    pre = jnp.dot(agg[...], weight[...], preferred_element_type=f32)
    root = math.sqrt(2.0 / math.pi)
    bend = jnp.tanh(root * (pre + 0.044715 * pre * pre * pre))
    act_out[...] = (0.5 * pre * (1.0 + bend)).astype(bf16)
    slope = 0.5 * (1.0 + bend) + 0.5 * pre * (1.0 - bend * bend) * (
        root * (1.0 + 3 * 0.044715 * pre * pre)
    )
    pre_grad = (cot[...].astype(f32) * slope).astype(bf16)
    row_grad = lax.dot_general(
        pre_grad, weight[...], (((1,), (1,)), ((), ())), preferred_element_type=f32
    )
    for s in range(parts):
        gbuf[s, quarter(rep), :] = row_grad[:, s * cols:(s + 1) * cols].astype(bf16)

    def g_copy(way, q, s):
        here = gbuf.at[s, quarter(q), :]
        return remote(here, here, g_send.at[way, s], g_recv.at[q, s], (over, mate, mate)[way])

    for s in range(parts):
        g_copy(0, rep, s).start()
    for s in range(parts):
        g_copy(1, rep, s).start()
    wacc[...] = lax.dot_general(
        agg[...], pre_grad, (((0,), (0,)), ((), ())), preferred_element_type=f32
    )
    half = wacc.shape[0] // 2
    strip = half // line

    def w_copy(step):
        src, dst, device = (
            (wcs, wcr, mate), (wys.at[1 - y], wyr, over), (wxs, wxr, across),
            (wfull.at[c, z, y], wfull.at[c, z, y], over), (wfull.at[c], wfull.at[c], mate),
        )[step]
        return remote(src, dst, w_send.at[step], w_recv.at[step], device)

    def w_arrival(step):
        dst = (wcr, wyr, wxr, wfull.at[c, z, 1 - y], wfull.at[1 - c])[step]
        remote(dst, dst, w_send.at[step], w_recv.at[step], mate).wait_recv()

    def wz_copy(k):
        other = (z + k) % line
        return remote(
            wzs.at[other], wzr.at[z], wz_send.at[k], wz_recv.at[z], (other * inner + x, rep)
        )

    def wz_wait(k):
        other = (z + k) % line
        remote(wzr.at[other], wzr.at[other], wz_send.at[k], wz_recv.at[other], across).wait_recv()

    def wa_copy(k):
        other = (z + k) % line
        here = wfull.at[c, z]
        return remote(here, here, wa_send.at[k], wa_recv.at[z], (other * inner + x, rep))

    def wa_wait(k):
        other = (z + k) % line
        there = wfull.at[c, other]
        remote(there, there, wa_send.at[k], wa_recv.at[other], across).wait_recv()

    def half_of(i):
        return pl.ds(pl.multiple_of(i * half, half), half)

    wcs[...] = wacc[half_of(1 - c), :].astype(bf16)
    w_copy(0).start()
    w_arrival(0)
    wzs[...] = (wacc[half_of(c), :] + wcr[...].astype(f32)).reshape(line, strip, width).astype(bf16)
    for k in range(1, line):
        wz_copy(k).start()

    def term_of(slot, s):
        return lax.dot_general(
            dense[slot], gbuf[s], (((0,), (0,)), ((), ())), preferred_element_type=f32
        )

    def x_copy(zz, s):
        return remote(xs.at[zz, s], xr.at[zz, s], x_send.at[zz, s], x_recv.at[zz, s], across)

    def send_across(s):
        @pl.loop(0, line)
        def _(i):
            d = line - 1 - i
            for zz, there in ((z + d, z + d < line), (z - d, (z - d >= 0) & (d > 0))):
                @pl.when(there)
                def _():
                    xs[zz, s] = term_of(zz * inner + 1 - x, s).astype(bf16)
                    x_copy(zz, s).start()

    def own_terms(s):
        @pl.loop(0, line)
        def _(zz):
            bown[zz, s] = term_of(zz * inner + x, s)

    def z_copy(zz, s, slot, device):
        return remote(zs.at[zz, s], zr.at[slot, s], z_send.at[zz, s], z_recv.at[slot, s], device)

    def z_wait(slot, s):
        remote(zr.at[slot, s], zr.at[slot, s], z_send.at[0, s], z_recv.at[slot, s], across).wait_recv()

    def pass_on(d, s):
        for zz, there, inflow, device, slot in (
            (z + d, z + d < line, z > 0, up, z + d),
            (z - d, z - d >= 0, z < line - 1, down, jnp.where(d == 1, line, z - d)),
        ):
            @pl.when(there)
            def _():
                x_copy(zz, s).wait_recv()
                bown[zz, s] += xr[zz, s].astype(f32)

                @pl.when(inflow)
                def _():
                    z_wait(zz, s)
                    bown[zz, s] += zr[zz, s].astype(f32)

                zs[zz, s] = bown[zz, s].astype(bf16)
                z_copy(zz, s, slot, device).start()

    def pass_rest(s):
        @pl.loop(1, line - 1)
        def _(i):
            pass_on(line - 1 - i, s)

    def finish(s):
        x_copy(z, s).wait_recv()
        bown[z, s] += xr[z, s].astype(f32)

        @pl.when(z > 0)
        def _():
            z_wait(z, s)
            bown[z, s] += zr[z, s].astype(f32)

        @pl.when(z < line - 1)
        def _():
            z_wait(line, s)
            bown[z, s] += zr[line, s].astype(f32)

        fg_out[:, s * cols:(s + 1) * cols] = bown[z, s].astype(bf16)

    def gather_grad(s):
        g_copy(1, y * 2 + 1 - c, s).wait_recv()
        g_copy(0, (1 - y) * 2 + c, s).wait_recv()
        g_copy(2, (1 - y) * 2 + c, s).start()

    def rest_of_grad(s):
        g_copy(2, (1 - y) * 2 + 1 - c, s).wait_recv()

    last = parts - 1
    for s in range(last):
        gather_grad(s)
        rest_of_grad(s)
        send_across(s)
        if s == 0:
            gather_grad(last)
        own_terms(s)
        pass_on(line - 1, s)
    for k in range(1, line):
        wz_wait(k)
    total = wzs[z].astype(f32)
    for k in range(1, line):
        total += wzr[(z + k) % line].astype(f32)
    wys[...] = total.reshape(2, strip // 2, width).astype(bf16)
    w_copy(1).start()
    rest_of_grad(last)
    w_arrival(1)
    wxs[...] = (wys[y].astype(f32) + wyr[...].astype(f32)).astype(bf16)
    w_copy(2).start()
    send_across(last)
    own_terms(last)
    for s in range(last):
        pass_rest(s)
    w_arrival(2)
    wfull[c, z, y] = ((wxs[...].astype(f32) + wxr[...].astype(f32)) * scale).astype(bf16)
    w_copy(3).start()
    for s in range(last):
        finish(s)
    pass_on(line - 1, last)
    w_arrival(3)
    for k in range(1, line):
        wa_copy(k).start()
    pass_rest(last)
    for k in range(1, line):
        wa_wait(k)
    w_copy(4).start()
    finish(last)
    w_arrival(4)
    wg_out[...] = wfull[...]

    @pl.loop(0, line)
    def _(zz):
        for s in range(parts):
            pl.when((zz <= z) & (z < line - 1))(lambda: ag_copy(0, zz, s).wait_send())
            pl.when((zz >= z) & (z > 0))(lambda: ag_copy(1, zz, s).wait_send())
            ag_copy(2, zz, s).wait_send()
            x_copy(zz, s).wait_send()
            pl.when(zz != z)(lambda: z_copy(zz, s, zz, across).wait_send())
    for s in range(parts):
        y_copy(s).wait_send()
        for qy in range(2):
            c_copy(qy, s).wait_send()
        for way in range(3):
            g_copy(way, rep, s).wait_send()
    for step in range(5):
        w_copy(step).wait_send()
    for k in range(1, line):
        wz_copy(k).wait_send()
        wa_copy(k).wait_send()


def finish_kernel(a_ref, w_ref, f_ref, a_out, w_out, f_out):
    a_out[...] = a_ref[...]
    w_out[...] = w_ref[...].astype(jnp.float32)
    f_out[...] = f_ref[...]


def layer(features, cotangent, weight, dense, scale, nodes):
    rows, width = features.shape
    inner = 2
    line = nodes // inner
    parts = 2
    cols = width // parts
    all_rows = dense.shape[1]
    half = width // 2
    strip = half // line
    bf16, f32, dma = jnp.bfloat16, jnp.float32, pltpu.SemaphoreType.DMA
    vmem = pl.BlockSpec(memory_space=pltpu.VMEM)
    shapes = [
        (dense.shape, bf16), ((nodes, parts, rows, cols), bf16), ((parts, all_rows, cols), f32),
        ((2, parts, rows, cols), bf16), ((2, parts, rows, cols), bf16),
        ((parts, rows, cols), bf16), ((parts, rows, cols), bf16),
        ((rows, width), bf16), ((parts, all_rows, cols), bf16), ((width, width), f32),
        ((half, width), bf16), ((half, width), bf16),
        ((strip // 2, width), bf16), ((strip // 2, width), bf16),
        ((2, strip // 2, width), bf16), ((strip // 2, width), bf16),
        ((line, strip, width), bf16), ((line, strip, width), bf16),
        ((2, line, 2, strip // 2, width), bf16),
        ((line, parts, rows, cols), f32), ((line, parts, rows, cols), bf16),
        ((line, parts, rows, cols), bf16), ((line, parts, rows, cols), bf16),
        ((line + 1, parts, rows, cols), bf16),
    ]
    sems = [
        dma, dma((3, line, parts)), dma((nodes, parts)), dma((2, parts)), dma((2, parts)),
        dma((parts,)), dma((parts,)), dma((3, parts)), dma((4, parts)), dma((5,)), dma((5,)),
        dma((line,)), dma((line,)), dma((line,)), dma((line,)),
        dma((line, parts)), dma((line, parts)), dma((line, parts)), dma((line + 1, parts)),
    ]
    activation, weight_grad, feature_grad = pl.pallas_call(
        functools.partial(layer_kernel, nodes, inner, scale),
        out_shape=(
            jax.ShapeDtypeStruct((rows, width), bf16),
            jax.ShapeDtypeStruct((2, line, 2, strip // 2, width), bf16),
            jax.ShapeDtypeStruct((rows, width), bf16),
        ),
        in_specs=[vmem] * 3 + [pl.BlockSpec(memory_space=pl.ANY)],
        out_specs=(vmem, vmem, vmem),
        scratch_shapes=[pltpu.VMEM(*shape) for shape in shapes] + sems,
        compiler_params=pltpu.CompilerParams(
            collective_id=0, has_side_effects=True, vmem_limit_bytes=63 << 20
        ),
        name="layer",
    )(features, cotangent, weight, dense)
    return pl.pallas_call(
        finish_kernel,
        out_shape=(
            jax.ShapeDtypeStruct((rows, width), bf16),
            jax.ShapeDtypeStruct((width, width), f32),
            jax.ShapeDtypeStruct((rows, width), bf16),
        ),
        in_specs=[vmem] * 3,
        out_specs=(vmem, vmem, vmem),
        name="finish",
    )(activation, weight_grad.reshape(width, width), feature_grad)


def local(features, weight, cotangent, tile_values, tile_row, tile_col, tile_count):
    rows_quarter = features.shape[0]
    rep_count = lax.axis_size("rep")
    node_count = lax.axis_size("node")
    scale = 1.0 / math.sqrt(rows_quarter * rep_count * node_count)
    subs = rows_quarter // TB
    blocks = subs * rep_count
    dense = densify(tile_values, tile_row, tile_col, tile_count, node_count, blocks, subs)
    return layer(features, cotangent, weight, dense, scale, node_count)


def solution(mesh):
    in_specs = (
        P(("node", "rep"), None),
        P(),
        P(("node", "rep"), None),
        P(("node", "rep"), None, None),
        P(("node", "rep")),
        P(("node", "rep")),
        P(("node", "rep")),
    )
    out_specs = (P(("node", "rep"), None), P(), P(("node", "rep"), None))
    return jax.shard_map(local, mesh=mesh, in_specs=in_specs, out_specs=out_specs, check_vma=False)
```

```python
import functools
import math

import jax
import jax.numpy as jnp
from jax import lax
from jax.experimental import pallas as pl
from jax.experimental.pallas import tpu as pltpu
from jax.sharding import PartitionSpec as P

TB = 128


def densify_kernel(blocks, subs, group, rows_ref, cols_ref, count_ref, tiles_ref, out_ref, acc, stage, sems):
    turn = pl.program_id(0)
    places = acc.shape[0] - 1
    nodes = places // (blocks * subs)

    @pl.when(turn == 0)
    def _():
        @pl.loop(0, places)
        def _(p):
            acc[p] = jnp.zeros((TB, TB), jnp.float32)

    count = count_ref[0]

    @pl.when(turn * group < count)
    def _():
        @pl.loop(0, group, unroll=True)
        def _(t):
            slot = turn * group + t
            col = cols_ref[slot]
            place = (col // subs * blocks + rows_ref[slot]) * subs + col % subs
            place = jnp.where(slot < count, place, places)
            acc[place] += tiles_ref[t].astype(jnp.float32)

    @pl.when(turn == pl.num_programs(0) - 1)
    def _():
        def copy_out(o):
            return pltpu.make_async_copy(stage.at[o % 2], out_ref.at[o], sems.at[o % 2])

        for o in range(nodes):
            if o >= 2:
                copy_out(o - 2).wait()
            for r in range(blocks):
                for s in range(subs):
                    stage[o % 2, r * TB:(r + 1) * TB, s * TB:(s + 1) * TB] = acc[
                        (o * blocks + r) * subs + s
                    ].astype(jnp.bfloat16)
            copy_out(o).start()
        for o in range(max(nodes - 2, 0), nodes):
            copy_out(o).wait()


def densify(tile_values, tile_row, tile_col, tile_count, nodes, blocks, subs):
    slots = tile_values.shape[0]
    group = math.gcd(slots, 32)
    places = nodes * blocks * subs

    def tile_block(i, rows, cols, count):
        return (jnp.minimum(i, (count[0] + group - 1) // group - 1), 0, 0)

    return pl.pallas_call(
        functools.partial(densify_kernel, blocks, subs, group),
        out_shape=jax.ShapeDtypeStruct((nodes, blocks * TB, subs * TB), jnp.bfloat16),
        grid_spec=pltpu.PrefetchScalarGridSpec(
            num_scalar_prefetch=3,
            grid=(slots // group,),
            in_specs=[pl.BlockSpec((group, TB, TB), tile_block)],
            out_specs=pl.BlockSpec(memory_space=pl.ANY),
            scratch_shapes=[
                pltpu.VMEM((places + 1, TB, TB), jnp.float32),
                pltpu.VMEM((2, blocks * TB, subs * TB), jnp.bfloat16),
                pltpu.SemaphoreType.DMA((2,)),
            ],
        ),
        compiler_params=pltpu.CompilerParams(vmem_limit_bytes=60 * 1024 * 1024),
        cost_estimate=pl.CostEstimate(
            flops=slots * TB * TB, bytes_accessed=4 * slots * TB * TB, transcendentals=0
        ),
        name="densify",
    )(tile_row, tile_col, tile_count, tile_values)


def layer_kernel(
    nodes, inner, scale, feat, cot, weight, dense_hbm, act_out, wg_out, fg_out,
    dense, turned, xbuf, acc, cs, cr, ys, yr, agg, gbuf, wacc, wcs, wcr, wxs, wxr, wys, wyr, wzs, wzr, wfull,
    bown, xs, xr, zs, zr,
    dense_sem, ag_send, ag_recv, c_send, c_recv, y_send, y_recv, g_send, g_recv,
    w_send, w_recv, wz_send, wz_recv, wa_send, wa_recv, x_send, x_recv, z_send, z_recv,
):
    line = nodes // inner
    parts = acc.shape[0]
    rows, width = feat.shape
    cols = width // parts
    node, rep = lax.axis_index("node"), lax.axis_index("rep")
    z, x = node // inner, node % inner
    y, c = rep // 2, rep % 2
    up, down, across = (node + inner, rep), (node - inner, rep), (z * inner + 1 - x, rep)
    mate, over = (node, y * 2 + 1 - c), (node, (1 - y) * 2 + c)
    bf16, f32 = jnp.bfloat16, jnp.float32

    def remote(src, dst, send, recv, device):
        return pltpu.make_async_remote_copy(
            src_ref=src, dst_ref=dst, send_sem=send, recv_sem=recv,
            device_id=device, device_id_type=pl.DeviceIdType.MESH,
        )

    load_dense = pltpu.make_async_copy(dense_hbm, dense, dense_sem)
    load_dense.start()

    barrier = pltpu.get_barrier_semaphore()
    for device in (across, mate, over):
        pl.semaphore_signal(barrier, inc=1, device_id=device, device_id_type=pl.DeviceIdType.MESH)
    for k in range(1, line):
        pl.semaphore_signal(
            barrier, inc=1, device_id=((z + k) % line * inner + x, rep),
            device_id_type=pl.DeviceIdType.MESH,
        )
    pl.semaphore_wait(barrier, 3 + line - 1)

    def ag_copy(way, zz, s, src=None):
        slot = zz * inner + x
        src = xbuf.at[slot, s] if src is None else src
        return remote(
            src, xbuf.at[slot, s], ag_send.at[way, zz, s], ag_recv.at[slot, s], (up, down, across)[way]
        )

    def ag_wait(slot, s):
        remote(xbuf.at[slot, s], xbuf.at[slot, s], ag_send.at[0, 0, s], ag_recv.at[slot, s], across).wait_recv()

    def columns(ref, s):
        return ref.at[:, s * cols:(s + 1) * cols]

    for s in range(parts):
        own = columns(feat, s)
        ag_copy(2, z, s, own).start()
        pl.when(z < line - 1)(lambda own=own, s=s: ag_copy(0, z, s, own).start())
        pl.when(z > 0)(lambda own=own, s=s: ag_copy(1, z, s, own).start())

    load_dense.wait()
    chunk = rows

    def multiply(slot, s, block, first=False):
        @pl.loop(0, acc.shape[1] // chunk)
        def _(i):
            here = pl.ds(pl.multiple_of(i * chunk, chunk), chunk)
            term = jnp.dot(dense[slot, here, :], block[...], preferred_element_type=f32)
            if first:
                acc[s, here, :] = term
            else:
                acc[s, here, :] += term

    for s in range(parts):
        multiply(node, s, columns(feat, s), True)

    @pl.loop(1, line)
    def _(d):
        low, high = z - d, z + d
        for s in range(parts):
            @pl.when(low >= 0)
            def _():
                ag_wait(low * inner + x, s)
                pl.when(z < line - 1)(lambda: ag_copy(0, low, s).start())
                ag_copy(2, low, s).start()

            @pl.when(high < line)
            def _():
                ag_wait(high * inner + x, s)
                pl.when(z > 0)(lambda: ag_copy(1, high, s).start())
                ag_copy(2, high, s).start()

        for zz, there in ((low, low >= 0), (high, high < line)):
            @pl.when(there)
            def _():
                for s in range(parts):
                    multiply(zz * inner + x, s, xbuf.at[zz * inner + x, s])

    def multiply_across(d, s):
        for zz, there in ((z - d, z - d >= 0), (z + d, (z + d < line) & (d > 0))):
            @pl.when(there)
            def _():
                slot = zz * inner + 1 - x
                ag_wait(slot, s)
                multiply(slot, s, xbuf.at[slot, s])

    @pl.loop(0, line - 1)
    def _(d):
        for s in range(parts):
            multiply_across(d, s)

    def quarter(q):
        return pl.ds(pl.multiple_of(q * rows, rows), rows)

    def c_copy(qy, s):
        return remote(cs.at[qy, s], cr.at[qy, s], c_send.at[qy, s], c_recv.at[qy, s], mate)

    def y_copy(s):
        return remote(ys.at[s], yr.at[s], y_send.at[s], y_recv.at[s], over)

    for s in range(parts):
        multiply_across(line - 1, s)
        for qy in (1 - y, y):
            cs[qy, s] = acc[s, quarter(qy * 2 + 1 - c), :].astype(bf16)
            c_copy(qy, s).start()
        c_copy(1 - y, s).wait_recv()
        ys[s] = (acc[s, quarter((1 - y) * 2 + c), :] + cr[1 - y, s].astype(f32)).astype(bf16)
        y_copy(s).start()
    turned_ready = turned.shape[0] == nodes

    def turn(side):
        if turned_ready:
            @pl.loop(0, line)
            def _(zz):
                turned[zz * inner + side] = dense[zz * inner + side].T

    turn(1 - x)
    for s in range(parts):
        c_copy(y, s).wait_recv()
        y_copy(s).wait_recv()
        total = acc[s, quarter(rep), :] + cr[y, s].astype(f32) + yr[s].astype(f32)
        agg[:, s * cols:(s + 1) * cols] = total.astype(bf16)

    pre = jnp.dot(agg[...], weight[...], preferred_element_type=f32)
    root = math.sqrt(2.0 / math.pi)
    bend = jnp.tanh(root * (pre + 0.044715 * pre * pre * pre))
    act_out[...] = (0.5 * pre * (1.0 + bend)).astype(bf16)
    slope = 0.5 * (1.0 + bend) + 0.5 * pre * (1.0 - bend * bend) * (
        root * (1.0 + 3 * 0.044715 * pre * pre)
    )
    pre_grad = (cot[...].astype(f32) * slope).astype(bf16)
    row_grad = lax.dot_general(
        pre_grad, weight[...], (((1,), (1,)), ((), ())), preferred_element_type=f32
    )
    for s in range(parts):
        gbuf[s, quarter(rep), :] = row_grad[:, s * cols:(s + 1) * cols].astype(bf16)

    def g_copy(way, q, s):
        here = gbuf.at[s, quarter(q), :]
        return remote(here, here, g_send.at[way, s], g_recv.at[q, s], (over, mate, mate)[way])

    for s in range(parts):
        g_copy(0, rep, s).start()
    for s in range(parts):
        g_copy(1, rep, s).start()
    wacc[...] = lax.dot_general(
        agg[...], pre_grad, (((0,), (0,)), ((), ())), preferred_element_type=f32
    )
    half = wacc.shape[0] // 2
    strip = half // line

    def w_copy(step):
        src, dst, device = (
            (wcs, wcr, mate), (wys.at[1 - y], wyr, over), (wxs, wxr, across),
            (wfull.at[c, z, y], wfull.at[c, z, y], over), (wfull.at[c], wfull.at[c], mate),
        )[step]
        return remote(src, dst, w_send.at[step], w_recv.at[step], device)

    def w_arrival(step):
        dst = (wcr, wyr, wxr, wfull.at[c, z, 1 - y], wfull.at[1 - c])[step]
        remote(dst, dst, w_send.at[step], w_recv.at[step], mate).wait_recv()

    def wz_copy(k):
        other = (z + k) % line
        return remote(
            wzs.at[other], wzr.at[z], wz_send.at[k], wz_recv.at[z], (other * inner + x, rep)
        )

    def wz_wait(k):
        other = (z + k) % line
        remote(wzr.at[other], wzr.at[other], wz_send.at[k], wz_recv.at[other], across).wait_recv()

    def wa_copy(k):
        other = (z + k) % line
        here = wfull.at[c, z]
        return remote(here, here, wa_send.at[k], wa_recv.at[z], (other * inner + x, rep))

    def wa_wait(k):
        other = (z + k) % line
        there = wfull.at[c, other]
        remote(there, there, wa_send.at[k], wa_recv.at[other], across).wait_recv()

    def half_of(i):
        return pl.ds(pl.multiple_of(i * half, half), half)

    wcs[...] = wacc[half_of(1 - c), :].astype(bf16)
    w_copy(0).start()
    w_arrival(0)
    wzs[...] = (wacc[half_of(c), :] + wcr[...].astype(f32)).reshape(line, strip, width).astype(bf16)
    for k in range(1, line):
        wz_copy(k).start()

    turn(x)

    def term_of(slot, s):
        if turned_ready:
            return jnp.dot(turned[slot], gbuf[s], preferred_element_type=f32)
        return lax.dot_general(
            dense[slot], gbuf[s], (((0,), (0,)), ((), ())), preferred_element_type=f32
        )

    def x_copy(zz, s):
        return remote(xs.at[zz, s], xr.at[zz, s], x_send.at[zz, s], x_recv.at[zz, s], across)

    def send_across(s):
        @pl.loop(0, line)
        def _(i):
            d = line - 1 - i
            for zz, there in ((z + d, z + d < line), (z - d, (z - d >= 0) & (d > 0))):
                @pl.when(there)
                def _():
                    xs[zz, s] = term_of(zz * inner + 1 - x, s).astype(bf16)
                    x_copy(zz, s).start()

    def own_terms(s):
        @pl.loop(0, line)
        def _(zz):
            bown[zz, s] = term_of(zz * inner + x, s)

    def z_copy(zz, s, slot, device):
        return remote(zs.at[zz, s], zr.at[slot, s], z_send.at[zz, s], z_recv.at[slot, s], device)

    def z_wait(slot, s):
        remote(zr.at[slot, s], zr.at[slot, s], z_send.at[0, s], z_recv.at[slot, s], across).wait_recv()

    def pass_on(d, s):
        for zz, there, inflow, device, slot in (
            (z + d, z + d < line, z > 0, up, z + d),
            (z - d, z - d >= 0, z < line - 1, down, jnp.where(d == 1, line, z - d)),
        ):
            @pl.when(there)
            def _():
                x_copy(zz, s).wait_recv()
                bown[zz, s] += xr[zz, s].astype(f32)

                @pl.when(inflow)
                def _():
                    z_wait(zz, s)
                    bown[zz, s] += zr[zz, s].astype(f32)

                zs[zz, s] = bown[zz, s].astype(bf16)
                z_copy(zz, s, slot, device).start()

    def pass_rest(s):
        @pl.loop(1, line - 1)
        def _(i):
            pass_on(line - 1 - i, s)

    def finish(s):
        x_copy(z, s).wait_recv()
        bown[z, s] += xr[z, s].astype(f32)

        @pl.when(z > 0)
        def _():
            z_wait(z, s)
            bown[z, s] += zr[z, s].astype(f32)

        @pl.when(z < line - 1)
        def _():
            z_wait(line, s)
            bown[z, s] += zr[line, s].astype(f32)

        fg_out[:, s * cols:(s + 1) * cols] = bown[z, s].astype(bf16)

    def gather_grad(s):
        g_copy(1, y * 2 + 1 - c, s).wait_recv()
        g_copy(0, (1 - y) * 2 + c, s).wait_recv()
        g_copy(2, (1 - y) * 2 + c, s).start()

    def rest_of_grad(s):
        g_copy(2, (1 - y) * 2 + 1 - c, s).wait_recv()

    last = parts - 1
    for s in range(last):
        gather_grad(s)
        rest_of_grad(s)
        send_across(s)
        if s == 0:
            gather_grad(last)
        own_terms(s)
        pass_on(line - 1, s)
    for k in range(1, line):
        wz_wait(k)
    total = wzs[z].astype(f32)
    for k in range(1, line):
        total += wzr[(z + k) % line].astype(f32)
    wys[...] = total.reshape(2, strip // 2, width).astype(bf16)
    w_copy(1).start()
    rest_of_grad(last)
    w_arrival(1)
    wxs[...] = (wys[y].astype(f32) + wyr[...].astype(f32)).astype(bf16)
    w_copy(2).start()
    send_across(last)
    own_terms(last)
    for s in range(last):
        pass_rest(s)
    w_arrival(2)
    wfull[c, z, y] = ((wxs[...].astype(f32) + wxr[...].astype(f32)) * scale).astype(bf16)
    w_copy(3).start()
    for s in range(last):
        finish(s)
    pass_on(line - 1, last)
    w_arrival(3)
    for k in range(1, line):
        wa_copy(k).start()
    pass_rest(last)
    for k in range(1, line):
        wa_wait(k)
    w_copy(4).start()
    finish(last)
    w_arrival(4)
    wg_out[...] = wfull[...]

    @pl.loop(0, line)
    def _(zz):
        for s in range(parts):
            pl.when((zz <= z) & (z < line - 1))(lambda: ag_copy(0, zz, s).wait_send())
            pl.when((zz >= z) & (z > 0))(lambda: ag_copy(1, zz, s).wait_send())
            ag_copy(2, zz, s).wait_send()
            x_copy(zz, s).wait_send()
            pl.when(zz != z)(lambda: z_copy(zz, s, zz, across).wait_send())
    for s in range(parts):
        y_copy(s).wait_send()
        for qy in range(2):
            c_copy(qy, s).wait_send()
        for way in range(3):
            g_copy(way, rep, s).wait_send()
    for step in range(5):
        w_copy(step).wait_send()
    for k in range(1, line):
        wz_copy(k).wait_send()
        wa_copy(k).wait_send()


def finish_kernel(a_ref, w_ref, f_ref, a_out, w_out, f_out):
    a_out[...] = a_ref[...]
    w_out[...] = w_ref[...].astype(jnp.float32)
    f_out[...] = f_ref[...]


def layer(features, cotangent, weight, dense, scale, nodes):
    rows, width = features.shape
    inner = 2
    line = nodes // inner
    parts = 2
    cols = width // parts
    all_rows = dense.shape[1]
    half = width // 2
    strip = half // line
    bf16, f32, dma = jnp.bfloat16, jnp.float32, pltpu.SemaphoreType.DMA
    vmem = pl.BlockSpec(memory_space=pltpu.VMEM)
    flipped = (nodes, dense.shape[2], all_rows) if dense.size < 4 << 20 else (1, 16, 128)
    shapes = [
        (dense.shape, bf16), (flipped, bf16), ((nodes, parts, rows, cols), bf16), ((parts, all_rows, cols), f32),
        ((2, parts, rows, cols), bf16), ((2, parts, rows, cols), bf16),
        ((parts, rows, cols), bf16), ((parts, rows, cols), bf16),
        ((rows, width), bf16), ((parts, all_rows, cols), bf16), ((width, width), f32),
        ((half, width), bf16), ((half, width), bf16),
        ((strip // 2, width), bf16), ((strip // 2, width), bf16),
        ((2, strip // 2, width), bf16), ((strip // 2, width), bf16),
        ((line, strip, width), bf16), ((line, strip, width), bf16),
        ((2, line, 2, strip // 2, width), bf16),
        ((line, parts, rows, cols), f32), ((line, parts, rows, cols), bf16),
        ((line, parts, rows, cols), bf16), ((line, parts, rows, cols), bf16),
        ((line + 1, parts, rows, cols), bf16),
    ]
    sems = [
        dma, dma((3, line, parts)), dma((nodes, parts)), dma((2, parts)), dma((2, parts)),
        dma((parts,)), dma((parts,)), dma((3, parts)), dma((4, parts)), dma((5,)), dma((5,)),
        dma((line,)), dma((line,)), dma((line,)), dma((line,)),
        dma((line, parts)), dma((line, parts)), dma((line, parts)), dma((line + 1, parts)),
    ]
    activation, weight_grad, feature_grad = pl.pallas_call(
        functools.partial(layer_kernel, nodes, inner, scale),
        out_shape=(
            jax.ShapeDtypeStruct((rows, width), bf16),
            jax.ShapeDtypeStruct((2, line, 2, strip // 2, width), bf16),
            jax.ShapeDtypeStruct((rows, width), bf16),
        ),
        in_specs=[vmem] * 3 + [pl.BlockSpec(memory_space=pl.ANY)],
        out_specs=(vmem, vmem, vmem),
        scratch_shapes=[pltpu.VMEM(*shape) for shape in shapes] + sems,
        compiler_params=pltpu.CompilerParams(
            collective_id=0, has_side_effects=True, vmem_limit_bytes=63 << 20
        ),
        name="layer",
    )(features, cotangent, weight, dense)
    return pl.pallas_call(
        finish_kernel,
        out_shape=(
            jax.ShapeDtypeStruct((rows, width), bf16),
            jax.ShapeDtypeStruct((width, width), f32),
            jax.ShapeDtypeStruct((rows, width), bf16),
        ),
        in_specs=[vmem] * 3,
        out_specs=(vmem, vmem, vmem),
        name="finish",
    )(activation, weight_grad.reshape(width, width), feature_grad)


def local(features, weight, cotangent, tile_values, tile_row, tile_col, tile_count):
    rows_quarter = features.shape[0]
    rep_count = lax.axis_size("rep")
    node_count = lax.axis_size("node")
    scale = 1.0 / math.sqrt(rows_quarter * rep_count * node_count)
    subs = rows_quarter // TB
    blocks = subs * rep_count
    dense = densify(tile_values, tile_row, tile_col, tile_count, node_count, blocks, subs)
    return layer(features, cotangent, weight, dense, scale, node_count)


def solution(mesh):
    in_specs = (
        P(("node", "rep"), None),
        P(),
        P(("node", "rep"), None),
        P(("node", "rep"), None, None),
        P(("node", "rep")),
        P(("node", "rep")),
        P(("node", "rep")),
    )
    out_specs = (P(("node", "rep"), None), P(), P(("node", "rep"), None))
    return jax.shard_map(local, mesh=mesh, in_specs=in_specs, out_specs=out_specs, check_vma=False)
```
